32 devices in a mesh: grp: 4 (over x, core), dp: 8 (over z, y).
Axes of the slice: x: 2, y: 2, z: 4, core: 2. Of those that a mesh axis runs over, the one named last changes fastest.
Arguments:
- query: bfloat16 [8, 512, 2560], P('dp', 'grp'), may hold values from -30 to 30
- resp_kv: bfloat16 [8, 512, 1024], P('dp', 'grp'), may hold values from -6 to 6
- prefix_kv: bfloat16 [8, 64, 1024], P('dp', 'grp'), may hold values from -30 to 30
- query_bias: float32 [2560], replicated, may hold values from -3 to 3
- kv_bias: float32 [1024], replicated, may hold values from -3 to 3
- out_grad: bfloat16 [8, 512, 2560], P('dp', 'grp'), may hold values from -6 to 6
- lengths: int32 [8, 4], P('dp', 'grp'), may hold values from 32 to 128
Outputs:
- attended: bfloat16 [8, 512, 2560], P('dp', 'grp')
- query_grad: bfloat16 [8, 512, 2560], P('dp', 'grp')
- resp_kv_grad: bfloat16 [8, 512, 1024], P('dp', 'grp')
- prefix_kv_grad: bfloat16 [8, 64, 1024], P('dp', 'grp')
- query_bias_grad: float32 [2560], replicated
- kv_bias_grad: float32 [1024], replicated
The draws below stay inside these ranges and needn't reach their ends.
All inputs are finite; a program needn't handle non-finite values.
Results may differ from the reference program's by a relative error of at most 0.013.
The reference program's roundings to bfloat16 on the way count: a program that leaves them out, or rounds other values in their place, can miss the bound.
Values may be sent and summed in bfloat16 or wider, within the bound.
A program may use at most 64 MiB of HBM per device.

```python
import jax
import jax.numpy as jnp
from jax import lax

QH = 20
KVH = 4
HD = 128
RESP = 128
PRE = 64
RESP_ALL = 512
PROMPTS = 8
N_GRP = 4


def make_pair(key):
    base = jax.random.fold_in(key, 7)
    first, second = jax.random.split(base, 2)
    queries = jax.random.normal(first, (PROMPTS, RESP_ALL, QH * HD), jnp.float32)
    prefix = jax.random.normal(second, (PROMPTS, PRE, 2 * KVH * HD), jnp.float32)
    return (jnp.clip(queries, -6.0, 6.0), jnp.clip(prefix, -6.0, 6.0))


def draw_query(key, part):
    return make_pair(key)[0].astype(jnp.bfloat16)


def draw_prefix_kv(key, part):
    return make_pair(key)[1].astype(jnp.bfloat16)


def plant(values, rng, low, high):
    place = [jax.random.randint(jax.random.fold_in(rng, axis), (), 0, length) for axis, length in enumerate(values.shape)]
    main_axis = values.shape.index(max(values.shape))
    beside = place[:main_axis] + [(place[main_axis] + 1) % values.shape[main_axis]] + place[main_axis + 1:]
    return values.at[tuple(place)].set(low).at[tuple(beside)].set(high)


def shard_levels(stream_key, extent, cuts, low, top_value):
    gain, own = 1.0, jax.random.fold_in(stream_key, 6)
    for dim, parts in cuts:
        heights = jnp.exp(jax.random.uniform(jax.random.fold_in(own, dim), (parts,), jnp.float32, low / len(cuts), top_value / len(cuts)))
        gain = gain * jnp.repeat(heights, extent[dim] // parts).reshape([-1 if axis == dim else 1 for axis in range(len(extent))])
    return gain


def normal_values(own_key, shape, deviation, limit, cuts=(), kind=jnp.bfloat16):
    entries = jax.random.normal(own_key, shape, jnp.float32) * deviation
    if len(cuts) > 0:
        entries = shard_levels(own_key, shape, cuts, -0.22, 0.18) * entries
    return jnp.clip(entries, min=-limit, max=limit).astype(kind)


def setup_inputs(seed: int = 0) -> dict:
    splits = jax.random.split(jax.random.key(seed), 8)
    return {
        "query": draw_query(jax.random.fold_in(splits[7], 71), 0),
        "resp_kv": normal_values(splits[1], (PROMPTS, RESP_ALL, 2 * KVH * HD), 1.0, 6.0, ((0, 8), (1, 4))),
        "prefix_kv": draw_prefix_kv(jax.random.fold_in(splits[7], 71), 0),
        "query_bias": normal_values(splits[3], (QH * HD,), 0.5, 3.0, (), jnp.float32),
        "kv_bias": normal_values(splits[4], (2 * KVH * HD,), 0.5, 3.0, (), jnp.float32),
        "out_grad": normal_values(splits[5], (PROMPTS, RESP_ALL, QH * HD), 1.0, 6.0, ((0, 8), (1, 4))),
        "lengths": plant(jax.random.randint(splits[6], (PROMPTS, N_GRP), RESP // 4, RESP + 1), jax.random.fold_in(splits[6], 1), RESP // 4, RESP).astype(jnp.int32),
    }


NEG_BIG = -1e30


def attend_group(queries, cotangent, key_blocks, value_blocks, allows):
    factor = queries.shape[-1] ** -0.5
    query_f = queries.astype(jnp.float32)
    grad_f = cotangent.astype(jnp.float32)
    scores = []
    for keys, allow in zip(key_blocks, allows):
        raw = jnp.einsum("thd,sd->hts", query_f, keys.astype(jnp.float32)) * factor
        scores.append(jnp.where(allow[None], raw, NEG_BIG))
    highest = jnp.max(scores[0], -1, keepdims=True)
    for item in scores[1:]:
        highest = jnp.maximum(highest, jnp.max(item, -1, keepdims=True))
    powers = [jnp.exp(item - highest) for item in scores]
    totals = sum(jnp.sum(item, -1, keepdims=True) for item in powers)
    chances = [item / totals for item in powers]
    rounded = [item.astype(jnp.bfloat16) for item in chances]
    output = sum(jnp.einsum("hts,sd->thd", wts.astype(jnp.float32), vals.astype(jnp.float32)) for wts, vals in zip(rounded, value_blocks))
    slopes = [jnp.einsum("thd,sd->hts", grad_f, vals.astype(jnp.float32)) for vals in value_blocks]
    row_dot = sum(jnp.sum(prob * slope, -1, keepdims=True) for prob, slope in zip(chances, slopes))
    shifted = [(prob * (slope - row_dot)).astype(jnp.bfloat16) for prob, slope in zip(chances, slopes)]
    query_grad = sum(jnp.einsum("hts,sd->thd", dsb.astype(jnp.float32), keys.astype(jnp.float32)) for dsb, keys in zip(shifted, key_blocks)) * factor
    key_grads = [jnp.einsum("hts,thd->sd", dsb.astype(jnp.float32), query_f) * factor for dsb in shifted]
    value_grads = [jnp.einsum("hts,thd->sd", wts.astype(jnp.float32), grad_f) for wts in rounded]
    return output, query_grad, key_grads, value_grads


def one_response(query, resp_kv, prefix, cotangent, length, query_bias, kv_bias):
    slots = query.shape[0]
    pre_rows = prefix.shape[0]
    group = QH // KVH
    width = KVH * HD
    biased_query = (query.astype(jnp.float32) + query_bias).astype(jnp.bfloat16)
    own_kv = (resp_kv.astype(jnp.float32) + kv_bias).astype(jnp.bfloat16)
    position = jnp.arange(slots, dtype=jnp.int32)
    live = position < length
    grad_live = jnp.where(live[:, None], cotangent, jnp.zeros_like(cotangent))
    allow_own = position[None, :] <= position[:, None]
    allow_pre = jnp.ones((slots, pre_rows), dtype=bool)
    queries = biased_query.reshape(slots, KVH, group, HD).transpose(1, 0, 2, 3)
    grads = grad_live.reshape(slots, KVH, group, HD).transpose(1, 0, 2, 3)
    pre_keys = prefix[:, :width].reshape(pre_rows, KVH, HD).transpose(1, 0, 2)
    pre_vals = prefix[:, width:].reshape(pre_rows, KVH, HD).transpose(1, 0, 2)
    own_keys = own_kv[:, :width].reshape(slots, KVH, HD).transpose(1, 0, 2)
    own_vals = own_kv[:, width:].reshape(slots, KVH, HD).transpose(1, 0, 2)

    def per_group(pieces):
        qpart, gpart, pkey, pval, okey, oval = pieces
        output, qgrad, kgrads, vgrads = attend_group(qpart, gpart, [pkey, okey], [pval, oval], [allow_pre, allow_own])
        return output, qgrad, kgrads[0], vgrads[0], kgrads[1], vgrads[1]

    output, qgrad, pk_grad, pv_grad, ok_grad, ov_grad = lax.map(per_group, (queries, grads, pre_keys, pre_vals, own_keys, own_vals))
    output = output.transpose(1, 0, 2, 3).reshape(slots, QH * HD)
    attended = jnp.where(live[:, None], output, 0.0).astype(jnp.bfloat16)
    qgrad = qgrad.transpose(1, 0, 2, 3).reshape(slots, QH * HD)
    own_grad = jnp.concatenate([ok_grad.transpose(1, 0, 2).reshape(slots, width), ov_grad.transpose(1, 0, 2).reshape(slots, width)], -1)
    pre_grad = jnp.concatenate([pk_grad.transpose(1, 0, 2).reshape(pre_rows, width), pv_grad.transpose(1, 0, 2).reshape(pre_rows, width)], -1)
    return attended, qgrad, own_grad, pre_grad


def reference(query, resp_kv, prefix_kv, query_bias, kv_bias, out_grad, lengths):
    def prompt(pieces):
        qpart, rpart, ppart, gpart, lpart = pieces
        prefix = (ppart.astype(jnp.float32) + kv_bias).astype(jnp.bfloat16)
        qsplit = qpart.reshape(N_GRP, RESP, QH * HD)
        rsplit = rpart.reshape(N_GRP, RESP, 2 * KVH * HD)
        gsplit = gpart.reshape(N_GRP, RESP, QH * HD)

        def single(qone, rone, gone, lone):
            return one_response(qone, rone, prefix, gone, lone, query_bias, kv_bias)

        attended, qgrad, own_grad, pre_grad = jax.vmap(single)(qsplit, rsplit, gsplit, lpart)
        held = lax.optimization_barrier(pre_grad.astype(jnp.bfloat16))
        pre_sum = jnp.sum(held.astype(jnp.float32), 0).astype(jnp.bfloat16)
        qsum = jnp.sum(qgrad, (0, 1))
        kvsum = jnp.sum(own_grad, (0, 1)) + jnp.sum(pre_grad, (0, 1))
        return (attended.reshape(RESP_ALL, QH * HD), qgrad.astype(jnp.bfloat16).reshape(RESP_ALL, QH * HD),
                own_grad.astype(jnp.bfloat16).reshape(RESP_ALL, 2 * KVH * HD), pre_sum, qsum, kvsum)

    result = lax.map(prompt, (query, resp_kv, prefix_kv, out_grad, lengths))
    return result[0], result[1], result[2], result[3], jnp.sum(result[4], 0), jnp.sum(result[5], 0)
```

```python
import functools

import jax
import jax.numpy as jnp
from jax import lax
from jax.experimental import pallas as pl
from jax.experimental.pallas import tpu as pltpu
from jax.sharding import PartitionSpec as P

QH = 20
KVH = 4
HD = 128
NEG_BIG = -1e30
GROUP = QH // KVH
WIDTH = KVH * HD
GCOLS = GROUP * HD
MESH = pl.DeviceIdType.MESH
F32 = jnp.float32
BF16 = jnp.bfloat16

NT = (((1,), (1,)), ((), ()))
NN = (((1,), (0,)), ((), ()))
TN = (((0,), (0,)), ((), ()))


def dot(a, b, dims):
    return lax.dot_general(a, b, dims, preferred_element_type=F32)


def heads_down(x):
    return jnp.concatenate([x[:, h * HD:(h + 1) * HD] for h in range(GROUP)], axis=0)


def kernel(
    n_grp, n_dp, rows_per,
    len_ref, q_hbm, kv_hbm, pre_ref, qb_ref, kvb_ref, g_hbm,
    att_hbm, dq_hbm, dkv_hbm, dpre_ref, qsum_ref, kvsum_ref,
    q_s, g_s, kv_s, q2, g2, kv2, sown, dpown, pb_s, att_s, dq_s, dkv_s,
    pre_all, pg, pr, bs, br, b2, fin,
    in_sem, out_sem,
    ag_send, ag_recv, pg_send, pg_recv, ba_send, ba_recv, bb_send, bb_recv, bc_send, bc_recv,
):
    me = lax.axis_index("grp")
    my = lax.axis_index("dp")
    factor = HD ** (-0.5)
    slots = q_s.shape[0]
    own_rows = pre_ref.shape[0]
    pre_rows = n_grp * own_rows

    barrier = pltpu.get_barrier_semaphore()
    for off in range(1, n_grp):
        pl.semaphore_signal(barrier, inc=1, device_id={"grp": lax.rem(me + off, n_grp)}, device_id_type=MESH)
    for off in range(1, n_dp):
        pl.semaphore_signal(barrier, inc=1, device_id={"dp": lax.rem(my + off, n_dp)}, device_id_type=MESH)

    loads = [pltpu.make_async_copy(kv_hbm, kv_s, in_sem.at[0])]
    for j in range(KVH):
        cols = pl.ds(j * GCOLS, GCOLS)
        loads.append(pltpu.make_async_copy(q_hbm.at[:, cols], q_s.at[:, cols], in_sem.at[1 + 2 * j]))
        loads.append(pltpu.make_async_copy(g_hbm.at[:, cols], g_s.at[:, cols], in_sem.at[2 + 2 * j]))
    for item in loads:
        item.start()

    kvb = kvb_ref[...].reshape(1, 2 * WIDTH)
    pre_all[me] = (pre_ref[...].astype(F32) + kvb).astype(BF16)

    def exchange(axis, here, count, src, dst, send, recv):
        out = []
        for off in range(1, count):
            peer = lax.rem(here + off, count)
            out.append(pltpu.make_async_remote_copy(
                src_ref=src(peer), dst_ref=dst.at[here],
                send_sem=send.at[off - 1], recv_sem=recv.at[here],
                device_id={axis: peer}, device_id_type=MESH))
        return out

    def arrived(axis, here, count, src, dst, send, recv):
        for off in range(1, count):
            peer = lax.rem(here + off, count)
            pltpu.make_async_remote_copy(
                src_ref=src(peer), dst_ref=dst.at[peer],
                send_sem=send.at[off - 1], recv_sem=recv.at[peer],
                device_id={axis: peer}, device_id_type=MESH).wait_recv()

    ag = ("grp", me, n_grp, lambda peer: pre_all.at[me], pre_all, ag_send, ag_recv)
    ba = ("grp", me, n_grp, lambda peer: bs.at[peer], br, ba_send, ba_recv)
    rs = ("grp", me, n_grp, lambda peer: pg.at[peer], pr, pg_send, pg_recv)
    bb = ("dp", my, n_dp, lambda peer: b2.at[my], b2, bb_send, bb_recv)
    bc = ("grp", me, n_grp, lambda peer: fin.at[me], fin, bc_send, bc_recv)

    length = len_ref[0, 0]
    live_in = lax.broadcasted_iota(jnp.int32, (slots, GCOLS), 0) < length
    live_out = lax.broadcasted_iota(jnp.int32, (slots, HD), 0) < length
    key_at = lax.broadcasted_iota(jnp.int32, (slots, slots), 0)
    row_at = lax.broadcasted_iota(jnp.int32, (slots, slots), 1)
    allow = jnp.concatenate([key_at <= row_at] * GROUP, axis=1)

    pl.semaphore_wait(barrier, n_grp - 1 + n_dp - 1)
    ag_out = exchange(*ag)
    for item in ag_out:
        item.start()

    loads[0].wait()
    kv2[...] = (kv_s[...].astype(F32) + kvb).astype(BF16)
    qb = qb_ref[...].reshape(1, QH * HD)
    for j in range(KVH):
        cols = slice(j * GCOLS, (j + 1) * GCOLS)
        loads[1 + 2 * j].wait()
        loads[2 + 2 * j].wait()
        qj = heads_down((q_s[:, cols].astype(F32) + qb[:, cols]).astype(BF16))
        gj = g_s[:, cols]
        gj = heads_down(jnp.where(live_in, gj, jnp.zeros_like(gj)))
        q2[j] = qj
        g2[j] = gj
        raw = dot(kv2[:, j * HD:(j + 1) * HD], qj, NT) * factor
        sown[j] = jnp.where(allow, raw, NEG_BIG)
        dpown[j] = dot(kv2[:, WIDTH + j * HD:WIDTH + (j + 1) * HD], gj, NT)

    arrived(*ag)

    stores = []
    for j in range(KVH):
        cols = pl.ds(j * GCOLS, GCOLS)
        kc = slice(j * HD, (j + 1) * HD)
        vc = slice(WIDTH + j * HD, WIDTH + (j + 1) * HD)
        pk = pre_all[:, :, kc].reshape(pre_rows, HD)
        pv = pre_all[:, :, vc].reshape(pre_rows, HD)
        qj = q2[j]
        gj = g2[j]
        s_p = dot(pk, qj, NT) * factor
        s_o = sown[j]
        dp_p = dot(pv, gj, NT)
        dp_o = dpown[j]
        top = jnp.maximum(jnp.max(s_p, 0, keepdims=True), jnp.max(s_o, 0, keepdims=True))
        e_p = jnp.exp(s_p - top)
        e_o = jnp.exp(s_o - top)
        inv = 1.0 / (jnp.sum(e_p, 0, keepdims=True) + jnp.sum(e_o, 0, keepdims=True))
        p_p = e_p * inv
        p_o = e_o * inv
        row = jnp.sum(p_p * dp_p, 0, keepdims=True) + jnp.sum(p_o * dp_o, 0, keepdims=True)
        ds = jnp.concatenate([(p_p * (dp_p - row)).astype(BF16), (p_o * (dp_o - row)).astype(BF16)], axis=0)
        pb = jnp.concatenate([p_p.astype(BF16), p_o.astype(BF16)], axis=0)
        pb_s[j] = pb
        keys = jnp.concatenate([pk, kv2[:, kc]], axis=0)
        dk = dot(ds, qj, NN) * factor
        dv = dot(pb, gj, NN)
        dq = dot(ds, keys, TN) * factor
        for col, grad, base in ((kc, dk, QH), (vc, dv, QH + KVH)):
            rounded = grad.astype(BF16)
            pg[:, :, col] = rounded[:pre_rows].reshape(n_grp, own_rows, HD)
            dkv_s[:, col] = rounded[pre_rows:]
            at = base + j
            bs[at // rows_per, at % rows_per:at % rows_per + 1, :] = jnp.sum(grad, 0, keepdims=True)
        for h in range(GROUP):
            part = dq[h * slots:(h + 1) * slots]
            at = j * GROUP + h
            bs[at // rows_per, at % rows_per:at % rows_per + 1, :] = jnp.sum(part, 0, keepdims=True)
            dq_s[:, at * HD:(at + 1) * HD] = part.astype(BF16)
        stores.append(pltpu.make_async_copy(dq_s.at[:, cols], dq_hbm.at[:, cols], out_sem.at[1 + 2 * j]))
        stores[-1].start()

    ba_out = exchange(*ba)
    for item in ba_out:
        item.start()
    rs_out = exchange(*rs)
    for item in rs_out:
        item.start()
    stores.append(pltpu.make_async_copy(dkv_s, dkv_hbm, out_sem.at[0]))
    stores[-1].start()

    def forward(j):
        cols = pl.ds(j * GCOLS, GCOLS)
        pv = pre_all[:, :, WIDTH + j * HD:WIDTH + (j + 1) * HD].reshape(pre_rows, HD)
        vals = jnp.concatenate([pv, kv2[:, WIDTH + j * HD:WIDTH + (j + 1) * HD]], axis=0)
        out = dot(pb_s[j], vals, TN)
        for h in range(GROUP):
            at = j * GROUP + h
            att_s[:, at * HD:(at + 1) * HD] = jnp.where(live_out, out[h * slots:(h + 1) * slots], 0.0).astype(BF16)
        stores.append(pltpu.make_async_copy(att_s.at[:, cols], att_hbm.at[:, cols], out_sem.at[2 + 2 * j]))
        stores[-1].start()

    for j in range(KVH // 2):
        forward(j)

    arrived(*ba)
    br[me] = bs[me]
    total = br[0]
    for k in range(1, n_grp):
        total = total + br[k]
    b2[my] = total
    bb_out = exchange(*bb)
    for item in bb_out:
        item.start()

    for j in range(KVH // 2, KVH):
        forward(j)

    arrived(*rs)
    pr[me] = pg[me]
    acc = pr[0].astype(F32)
    for k in range(1, n_grp):
        acc = acc + pr[k].astype(F32)
    dpre_ref[...] = acc.astype(BF16)

    arrived(*bb)
    total = b2[0]
    for k in range(1, n_dp):
        total = total + b2[k]
    fin[me] = total
    bc_out = exchange(*bc)
    for item in bc_out:
        item.start()
    for item in stores:
        item.wait()
    for item in ag_out + ba_out + rs_out + bb_out:
        item.wait_send()
    arrived(*bc)
    for r in range(QH):
        qsum_ref[pl.ds(r * HD, HD)] = fin[r // rows_per, r % rows_per]
    for r in range(2 * KVH):
        at = QH + r
        kvsum_ref[pl.ds(r * HD, HD)] = fin[at // rows_per, at % rows_per]
    for item in bc_out:
        item.wait_send()


def local(n_grp, n_dp, query, resp_kv, prefix_kv, query_bias, kv_bias, out_grad, lengths):
    slots = query.shape[1]
    own_rows = prefix_kv.shape[1]
    pre_rows = own_rows * n_grp
    rows_per = -(-(QH + 2 * KVH) // n_grp)
    if n_grp * 8 >= QH + 2 * KVH:
        rows_per = min(8, 1 << (rows_per - 1).bit_length())
    tile = -(-rows_per // 8) * 8
    qw = QH * HD
    kw = 2 * WIDTH
    any_spec = pl.BlockSpec(memory_space=pl.ANY)
    vmem = pl.BlockSpec(memory_space=pltpu.VMEM)
    smem = pl.BlockSpec(memory_space=pltpu.SMEM)
    dma = lambda n: pltpu.SemaphoreType.DMA((n,))
    outs = pl.pallas_call(
        functools.partial(kernel, n_grp, n_dp, rows_per),
        name="replay",
        out_shape=(
            jax.ShapeDtypeStruct((slots, qw), BF16),
            jax.ShapeDtypeStruct((slots, qw), BF16),
            jax.ShapeDtypeStruct((slots, kw), BF16),
            jax.ShapeDtypeStruct((own_rows, kw), BF16),
            jax.ShapeDtypeStruct((qw,), F32),
            jax.ShapeDtypeStruct((kw,), F32),
        ),
        in_specs=[smem, any_spec, any_spec, vmem, vmem, vmem, any_spec],
        out_specs=(any_spec, any_spec, any_spec, vmem, vmem, vmem),
        scratch_shapes=[
            pltpu.VMEM((slots, qw), BF16),
            pltpu.VMEM((slots, qw), BF16),
            pltpu.VMEM((slots, kw), BF16),
            pltpu.VMEM((KVH, GROUP * slots, HD), BF16),
            pltpu.VMEM((KVH, GROUP * slots, HD), BF16),
            pltpu.VMEM((slots, kw), BF16),
            pltpu.VMEM((KVH, slots, GROUP * slots), F32),
            pltpu.VMEM((KVH, slots, GROUP * slots), F32),
            pltpu.VMEM((KVH, pre_rows + slots, GROUP * slots), BF16),
            pltpu.VMEM((slots, qw), BF16),
            pltpu.VMEM((slots, qw), BF16),
            pltpu.VMEM((slots, kw), BF16),
            pltpu.VMEM((n_grp, own_rows, kw), BF16),
            pltpu.VMEM((n_grp, own_rows, kw), BF16),
            pltpu.VMEM((n_grp, own_rows, kw), BF16),
            pltpu.VMEM((n_grp, tile, HD), F32),
            pltpu.VMEM((n_grp, tile, HD), F32),
            pltpu.VMEM((n_dp, tile, HD), F32),
            pltpu.VMEM((n_grp, tile, HD), F32),
            dma(1 + 2 * KVH), dma(1 + 2 * KVH),
            dma(n_grp - 1), dma(n_grp), dma(n_grp - 1), dma(n_grp),
            dma(n_grp - 1), dma(n_grp), dma(n_dp - 1), dma(n_dp),
            dma(n_grp - 1), dma(n_grp),
        ],
        compiler_params=pltpu.CompilerParams(
            collective_id=0, has_side_effects=True, vmem_limit_bytes=24 * 1024 * 1024
        ),
    )(lengths, query[0], resp_kv[0], prefix_kv[0], query_bias, kv_bias, out_grad[0])
    att, dq, dkv, dpre, qsum, kvsum = outs
    return att[None], dq[None], dkv[None], dpre[None], qsum, kvsum


def solution(mesh):
    return jax.shard_map(
        functools.partial(local, mesh.shape["grp"], mesh.shape["dp"]),
        mesh=mesh,
        in_specs=(
            P("dp", "grp", None),
            P("dp", "grp", None),
            P("dp", "grp", None),
            P(),
            P(),
            P("dp", "grp", None),
            P("dp", "grp"),
        ),
        out_specs=(
            P("dp", "grp", None),
            P("dp", "grp", None),
            P("dp", "grp", None),
            P("dp", "grp", None),
            P(),
            P(),
        ),
        check_vma=False,
    )
```

```python
import functools

import jax
import jax.numpy as jnp
from jax import lax
from jax.experimental import pallas as pl
from jax.experimental.pallas import tpu as pltpu
from jax.sharding import PartitionSpec as P

QH = 20
KVH = 4
HD = 128
NEG_BIG = -1e30
GROUP = QH // KVH
WIDTH = KVH * HD
GCOLS = GROUP * HD
MESH = pl.DeviceIdType.MESH
F32 = jnp.float32
BF16 = jnp.bfloat16

NT = (((1,), (1,)), ((), ()))
NN = (((1,), (0,)), ((), ()))
TN = (((0,), (0,)), ((), ()))


def dot(a, b, dims):
    return lax.dot_general(a, b, dims, preferred_element_type=F32)


def heads_down(x):
    return jnp.concatenate([x[:, h * HD:(h + 1) * HD] for h in range(GROUP)], axis=0)


def kernel(
    n_grp, n_dp, rows_per,
    len_ref, q_hbm, kv_hbm, pre_hbm, qb_hbm, kvb_hbm, g_hbm,
    att_s, dq_s, dkv_s, dpre_ref, qsum_ref, kvsum_ref,
    pre_ref, qb_ref, kvb_ref, q_s, g_s, kv_s, q2, g2, kv2, sown, dpown, pb_s,
    pre_all, pg, pr, bs, br, b2, fin,
    in_sem,
    ag_send, ag_recv, pg_send, pg_recv, ba_send, ba_recv, bb_send, bb_recv, bc_send, bc_recv,
):
    me = lax.axis_index("grp")
    my = lax.axis_index("dp")
    factor = HD ** (-0.5)
    slots = q_s.shape[0]
    own_rows = pre_ref.shape[0]
    pre_rows = n_grp * own_rows

    barrier = pltpu.get_barrier_semaphore()
    for off in range(1, n_grp):
        pl.semaphore_signal(barrier, inc=1, device_id={"grp": lax.rem(me + off, n_grp)}, device_id_type=MESH)
    for off in range(1, n_dp):
        pl.semaphore_signal(barrier, inc=1, device_id={"dp": lax.rem(my + off, n_dp)}, device_id_type=MESH)

    base = 1 + 2 * KVH
    small = [
        pltpu.make_async_copy(src, dst, in_sem.at[base + k])
        for k, (src, dst) in enumerate(
            ((pre_hbm, pre_ref), (kvb_hbm, kvb_ref), (qb_hbm, qb_ref)))
    ]
    loads = [pltpu.make_async_copy(kv_hbm, kv_s, in_sem.at[0])]
    for j in range(KVH):
        cols = pl.ds(j * GCOLS, GCOLS)
        loads.append(pltpu.make_async_copy(q_hbm.at[:, cols], q_s.at[:, cols], in_sem.at[1 + 2 * j]))
        loads.append(pltpu.make_async_copy(g_hbm.at[:, cols], g_s.at[:, cols], in_sem.at[2 + 2 * j]))
    for item in small + loads:
        item.start()
    small[0].wait()
    small[1].wait()
    kvb = kvb_ref[...].reshape(1, 2 * WIDTH)
    mine = (pre_ref[...].astype(F32) + kvb).astype(BF16)
    for j in range(KVH):
        pre_all[j, me] = jnp.concatenate(
            [mine[:, j * HD:(j + 1) * HD], mine[:, WIDTH + j * HD:WIDTH + (j + 1) * HD]], axis=1)
    small[2].wait()

    sent = []

    def exchange(axis, here, count, src, dst, send, recv):
        for off in range(1, count):
            peer = lax.rem(here + off, count)
            sent.append(pltpu.make_async_remote_copy(
                src_ref=src(peer), dst_ref=dst.at[here],
                send_sem=send.at[off - 1], recv_sem=recv.at[here],
                device_id={axis: peer}, device_id_type=MESH))
            sent[-1].start()

    def arrived(axis, here, count, src, dst, send, recv):
        for off in range(1, count):
            peer = lax.rem(here + off, count)
            pltpu.make_async_remote_copy(
                src_ref=src(peer), dst_ref=dst.at[peer],
                send_sem=send.at[off - 1], recv_sem=recv.at[peer],
                device_id={axis: peer}, device_id_type=MESH).wait_recv()

    ag = [("grp", me, n_grp, lambda peer, j=j: pre_all.at[j, me], pre_all.at[j], ag_send.at[j], ag_recv.at[j])
          for j in range(KVH)]
    rs = [("grp", me, n_grp, lambda peer, j=j: pg.at[j, peer], pr.at[j], pg_send.at[j], pg_recv.at[j])
          for j in range(KVH)]
    ba = ("grp", me, n_grp, lambda peer: bs.at[peer], br, ba_send, ba_recv)
    bb = ("dp", my, n_dp, lambda peer: b2.at[my], b2, bb_send, bb_recv)
    bc = ("grp", me, n_grp, lambda peer: fin.at[me], fin, bc_send, bc_recv)

    length = len_ref[0, 0]
    live_in = lax.broadcasted_iota(jnp.int32, (slots, GCOLS), 0) < length
    live_out = lax.broadcasted_iota(jnp.int32, (slots, HD), 0) < length
    key_at = lax.broadcasted_iota(jnp.int32, (slots, slots), 0)
    row_at = lax.broadcasted_iota(jnp.int32, (slots, slots), 1)
    allow = jnp.concatenate([key_at <= row_at] * GROUP, axis=1)

    loads[0].wait()
    kv2[...] = (kv_s[...].astype(F32) + kvb).astype(BF16)
    qb = qb_ref[...].reshape(1, QH * HD)
    def ready(j):
        cols = slice(j * GCOLS, (j + 1) * GCOLS)
        loads[1 + 2 * j].wait()
        loads[2 + 2 * j].wait()
        qj = heads_down((q_s[:, cols].astype(F32) + qb[:, cols]).astype(BF16))
        gj = g_s[:, cols]
        gj = heads_down(jnp.where(live_in, gj, jnp.zeros_like(gj)))
        q2[j] = qj
        g2[j] = gj
        raw = dot(kv2[:, j * HD:(j + 1) * HD], qj, NT) * factor
        sown[j] = jnp.where(allow, raw, NEG_BIG)
        dpown[j] = dot(kv2[:, WIDTH + j * HD:WIDTH + (j + 1) * HD], gj, NT)

    ready(0)
    pl.semaphore_wait(barrier, n_grp - 1 + n_dp - 1)
    for j in range(KVH):
        exchange(*ag[j])
    for j in range(1, KVH):
        ready(j)

    for j in range(KVH):
        arrived(*ag[j])
        kc = slice(j * HD, (j + 1) * HD)
        vc = slice(WIDTH + j * HD, WIDTH + (j + 1) * HD)
        both = pre_all[j].reshape(pre_rows, 2 * HD)
        pk = both[:, :HD]
        pv = both[:, HD:]
        qj = q2[j]
        gj = g2[j]
        s_p = dot(pk, qj, NT) * factor
        s_o = sown[j]
        dp_p = dot(pv, gj, NT)
        dp_o = dpown[j]
        top = jnp.maximum(jnp.max(s_p, 0, keepdims=True), jnp.max(s_o, 0, keepdims=True))
        e_p = jnp.exp(s_p - top)
        e_o = jnp.exp(s_o - top)
        inv = 1.0 / (jnp.sum(e_p, 0, keepdims=True) + jnp.sum(e_o, 0, keepdims=True))
        p_p = e_p * inv
        p_o = e_o * inv
        row = jnp.sum(p_p * dp_p, 0, keepdims=True) + jnp.sum(p_o * dp_o, 0, keepdims=True)
        ds = jnp.concatenate([(p_p * (dp_p - row)).astype(BF16), (p_o * (dp_o - row)).astype(BF16)], axis=0)
        pb = jnp.concatenate([p_p.astype(BF16), p_o.astype(BF16)], axis=0)
        pb_s[j] = pb
        keys = jnp.concatenate([pk, kv2[:, kc]], axis=0)
        dk = dot(ds, qj, NN) * factor
        dv = dot(pb, gj, NN)
        dq = dot(ds, keys, TN) * factor
        dkr = dk.astype(BF16)
        dvr = dv.astype(BF16)
        pg[j] = jnp.concatenate([dkr[:pre_rows], dvr[:pre_rows]], axis=1).reshape(n_grp, own_rows, 2 * HD)
        exchange(*rs[j])
        dkv_s[:, kc] = dkr[pre_rows:]
        dkv_s[:, vc] = dvr[pre_rows:]
        for at, grad in ((QH + j, dk), (QH + KVH + j, dv)):
            bs[at // rows_per, at % rows_per:at % rows_per + 1, :] = jnp.sum(grad, 0, keepdims=True)
        for h in range(GROUP):
            part = dq[h * slots:(h + 1) * slots]
            at = j * GROUP + h
            bs[at // rows_per, at % rows_per:at % rows_per + 1, :] = jnp.sum(part, 0, keepdims=True)
            dq_s[:, at * HD:(at + 1) * HD] = part.astype(BF16)

    exchange(*ba)

    def forward(j):
        pv = pre_all[j].reshape(pre_rows, 2 * HD)[:, HD:]
        vals = jnp.concatenate([pv, kv2[:, WIDTH + j * HD:WIDTH + (j + 1) * HD]], axis=0)
        out = dot(pb_s[j], vals, TN)
        for h in range(GROUP):
            at = j * GROUP + h
            att_s[:, at * HD:(at + 1) * HD] = jnp.where(live_out, out[h * slots:(h + 1) * slots], 0.0).astype(BF16)

    for j in range(KVH // 2):
        forward(j)

    arrived(*ba)
    br[me] = bs[me]
    total = br[0]
    for k in range(1, n_grp):
        total = total + br[k]
    b2[my] = total
    exchange(*bb)

    for j in range(KVH // 2, KVH):
        forward(j)

    for j in range(KVH):
        arrived(*rs[j])
        pr[j, me] = pg[j, me]
        acc = pr[j, 0].astype(F32)
        for k in range(1, n_grp):
            acc = acc + pr[j, k].astype(F32)
        acc = acc.astype(BF16)
        dpre_ref[:, j * HD:(j + 1) * HD] = acc[:, :HD]
        dpre_ref[:, WIDTH + j * HD:WIDTH + (j + 1) * HD] = acc[:, HD:]

    arrived(*bb)
    total = b2[0]
    for k in range(1, n_dp):
        total = total + b2[k]
    fin[me] = total
    exchange(*bc)
    for item in sent:
        item.wait_send()
    arrived(*bc)
    for r in range(QH):
        qsum_ref[pl.ds(r * HD, HD)] = fin[r // rows_per, r % rows_per]
    for r in range(2 * KVH):
        at = QH + r
        kvsum_ref[pl.ds(r * HD, HD)] = fin[at // rows_per, at % rows_per]


def write_out(*refs):
    count = (len(refs) - 1) // 2
    copies = [pltpu.make_async_copy(refs[k], refs[count + k], refs[-1].at[k]) for k in range(count)]
    for item in copies:
        item.start()
    for item in copies:
        item.wait()


def local(n_grp, n_dp, query, resp_kv, prefix_kv, query_bias, kv_bias, out_grad, lengths):
    slots = query.shape[1]
    own_rows = prefix_kv.shape[1]
    pre_rows = own_rows * n_grp
    rows_per = -(-(QH + 2 * KVH) // n_grp)
    if n_grp * 8 >= QH + 2 * KVH:
        rows_per = min(8, 1 << (rows_per - 1).bit_length())
    tile = -(-rows_per // 8) * 8
    qw = QH * HD
    kw = 2 * WIDTH
    hbm = pl.BlockSpec(memory_space=pltpu.HBM)
    vmem = pl.BlockSpec(memory_space=pltpu.VMEM)
    dma = lambda *n: pltpu.SemaphoreType.DMA(n)
    shapes = (
        jax.ShapeDtypeStruct((slots, qw), BF16),
        jax.ShapeDtypeStruct((slots, qw), BF16),
        jax.ShapeDtypeStruct((slots, kw), BF16),
        jax.ShapeDtypeStruct((own_rows, kw), BF16),
        jax.ShapeDtypeStruct((qw,), F32),
        jax.ShapeDtypeStruct((kw,), F32),
    )
    outs = pl.pallas_call(
        functools.partial(kernel, n_grp, n_dp, rows_per),
        name="replay",
        out_shape=shapes,
        in_specs=[pl.BlockSpec(memory_space=pltpu.SMEM)] + [hbm] * 6,
        out_specs=(vmem,) * 6,
        scratch_shapes=[
            pltpu.VMEM((own_rows, kw), BF16),
            pltpu.VMEM((qw,), F32),
            pltpu.VMEM((kw,), F32),
            pltpu.VMEM((slots, qw), BF16),
            pltpu.VMEM((slots, qw), BF16),
            pltpu.VMEM((slots, kw), BF16),
            pltpu.VMEM((KVH, GROUP * slots, HD), BF16),
            pltpu.VMEM((KVH, GROUP * slots, HD), BF16),
            pltpu.VMEM((slots, kw), BF16),
            pltpu.VMEM((KVH, slots, GROUP * slots), F32),
            pltpu.VMEM((KVH, slots, GROUP * slots), F32),
            pltpu.VMEM((KVH, pre_rows + slots, GROUP * slots), BF16),
            pltpu.VMEM((KVH, n_grp, own_rows, 2 * HD), BF16),
            pltpu.VMEM((KVH, n_grp, own_rows, 2 * HD), BF16),
            pltpu.VMEM((KVH, n_grp, own_rows, 2 * HD), BF16),
            pltpu.VMEM((n_grp, tile, HD), F32),
            pltpu.VMEM((n_grp, tile, HD), F32),
            pltpu.VMEM((n_dp, tile, HD), F32),
            pltpu.VMEM((n_grp, tile, HD), F32),
            dma(4 + 2 * KVH),
            dma(KVH, n_grp - 1), dma(KVH, n_grp), dma(KVH, n_grp - 1), dma(KVH, n_grp),
            dma(n_grp - 1), dma(n_grp), dma(n_dp - 1), dma(n_dp),
            dma(n_grp - 1), dma(n_grp),
        ],
        compiler_params=pltpu.CompilerParams(
            collective_id=0, has_side_effects=True, vmem_limit_bytes=24 * 1024 * 1024
        ),
    )(lengths, *(pltpu.with_memory_space_constraint(x, pltpu.HBM) for x in (query[0], resp_kv[0], prefix_kv[0], query_bias, kv_bias, out_grad[0])))
    att, dq, dkv, dpre, qsum, kvsum = pl.pallas_call(
        write_out,
        name="write_out",
        out_shape=shapes,
        in_specs=[vmem] * 6,
        out_specs=(hbm,) * 6,
        scratch_shapes=[dma(6)],
        compiler_params=pltpu.CompilerParams(vmem_limit_bytes=1024 * 1024),
    )(*outs)
    return att[None], dq[None], dkv[None], dpre[None], qsum, kvsum


def solution(mesh):
    return jax.shard_map(
        functools.partial(local, mesh.shape["grp"], mesh.shape["dp"]),
        mesh=mesh,
        in_specs=(
            P("dp", "grp", None),
            P("dp", "grp", None),
            P("dp", "grp", None),
            P(),
            P(),
            P("dp", "grp", None),
            P("dp", "grp"),
        ),
        out_specs=(
            P("dp", "grp", None),
            P("dp", "grp", None),
            P("dp", "grp", None),
            P("dp", "grp", None),
            P(),
            P(),
        ),
        check_vma=False,
    )
```

```python
import functools

import jax
import jax.numpy as jnp
from jax import lax
from jax.experimental import pallas as pl
from jax.experimental.pallas import tpu as pltpu
from jax.sharding import PartitionSpec as P

QH = 20
KVH = 4
STEP = 2
HD = 128
NEG_BIG = -1e30
GROUP = QH // KVH
WIDTH = KVH * HD
GCOLS = GROUP * HD
MESH = pl.DeviceIdType.MESH
F32 = jnp.float32
BF16 = jnp.bfloat16

NT = (((1,), (1,)), ((), ()))
NN = (((1,), (0,)), ((), ()))
TN = (((0,), (0,)), ((), ()))


def dot(a, b, dims):
    return lax.dot_general(a, b, dims, preferred_element_type=F32)


def heads_down(x):
    return jnp.concatenate([x[:, h * HD:(h + 1) * HD] for h in range(GROUP)], axis=0)


def kernel(
    n_grp, n_dp, rows_per,
    len_ref, q_hbm, kv_hbm, pre_hbm, qb_hbm, kvb_hbm, g_hbm,
    att_s, dq_s, dkv_s, dpre_ref, qsum_ref, kvsum_ref,
    pre_ref, qb_ref, kvb_ref, q_s, g_s, kv_s, q2, g2, kv2, sown, dpown, pb_s,
    pre_all, pg, pr, bs, br, b2, fin,
    in_sem,
    ag_send, ag_recv, pg_send, pg_recv, ba_send, ba_recv, bb_send, bb_recv, bc_send, bc_recv,
):
    me = lax.axis_index("grp")
    my = lax.axis_index("dp")
    factor = HD ** (-0.5)
    slots = q_s.shape[0]
    own_rows = pre_ref.shape[0]
    pre_rows = n_grp * own_rows

    barrier = pltpu.get_barrier_semaphore()
    for off in range(1, n_grp):
        pl.semaphore_signal(barrier, inc=1, device_id={"grp": lax.rem(me + off, n_grp)}, device_id_type=MESH)
    for off in range(1, n_dp):
        pl.semaphore_signal(barrier, inc=1, device_id={"dp": lax.rem(my + off, n_dp)}, device_id_type=MESH)

    base = 1 + 2 * KVH
    small = [
        pltpu.make_async_copy(src, dst, in_sem.at[base + k])
        for k, (src, dst) in enumerate(
            ((pre_hbm, pre_ref), (kvb_hbm, kvb_ref), (qb_hbm, qb_ref)))
    ]
    loads = [pltpu.make_async_copy(kv_hbm, kv_s, in_sem.at[0])]
    for j in range(KVH):
        cols = pl.ds(j * GCOLS, GCOLS)
        loads.append(pltpu.make_async_copy(q_hbm.at[:, cols], q_s.at[:, cols], in_sem.at[1 + 2 * j]))
        loads.append(pltpu.make_async_copy(g_hbm.at[:, cols], g_s.at[:, cols], in_sem.at[2 + 2 * j]))
    for item in small + loads:
        item.start()
    small[0].wait()
    small[1].wait()
    kvb = kvb_ref[...].reshape(1, 2 * WIDTH)
    mine = (pre_ref[...].astype(F32) + kvb).astype(BF16)
    for j in range(KVH):
        pre_all[j, me] = jnp.concatenate(
            [mine[:, j * HD:(j + 1) * HD], mine[:, WIDTH + j * HD:WIDTH + (j + 1) * HD]], axis=1)
    small[2].wait()

    sent = []

    def exchange(axis, here, count, src, dst, send, recv):
        for off in range(1, count):
            peer = lax.rem(here + off, count)
            sent.append(pltpu.make_async_remote_copy(
                src_ref=src(peer), dst_ref=dst.at[here],
                send_sem=send.at[off - 1], recv_sem=recv.at[here],
                device_id={axis: peer}, device_id_type=MESH))
            sent[-1].start()

    def arrived(axis, here, count, src, dst, send, recv):
        for off in range(1, count):
            peer = lax.rem(here + off, count)
            pltpu.make_async_remote_copy(
                src_ref=src(peer), dst_ref=dst.at[peer],
                send_sem=send.at[off - 1], recv_sem=recv.at[peer],
                device_id={axis: peer}, device_id_type=MESH).wait_recv()

    ag = [("grp", me, n_grp, lambda peer, j=j: pre_all.at[j, me], pre_all.at[j], ag_send.at[j], ag_recv.at[j])
          for j in range(KVH)]
    rs = [("grp", me, n_grp, lambda peer, j=j: pg.at[j, peer], pr.at[j], pg_send.at[j], pg_recv.at[j])
          for j in range(KVH)]
    ba = ("grp", me, n_grp, lambda peer: bs.at[peer], br, ba_send, ba_recv)
    bb = ("dp", my, n_dp, lambda peer: b2.at[my], b2, bb_send, bb_recv)
    bc = ("grp", me, n_grp, lambda peer: fin.at[me], fin, bc_send, bc_recv)

    length = len_ref[0, 0]
    live_in = lax.broadcasted_iota(jnp.int32, (slots, GCOLS), 0) < length
    live_out = lax.broadcasted_iota(jnp.int32, (slots, HD), 0) < length
    key_at = lax.broadcasted_iota(jnp.int32, (slots, slots), 0)
    row_at = lax.broadcasted_iota(jnp.int32, (slots, slots), 1)
    allow = jnp.concatenate([key_at <= row_at] * GROUP, axis=1)

    loads[0].wait()
    kv2[...] = (kv_s[...].astype(F32) + kvb).astype(BF16)
    qb = qb_ref[...].reshape(1, QH * HD)
    def ready(j):
        cols = slice(j * GCOLS, (j + 1) * GCOLS)
        loads[1 + 2 * j].wait()
        loads[2 + 2 * j].wait()
        qj = heads_down((q_s[:, cols].astype(F32) + qb[:, cols]).astype(BF16))
        gj = g_s[:, cols]
        gj = heads_down(jnp.where(live_in, gj, jnp.zeros_like(gj)))
        q2[j] = qj
        g2[j] = gj
        raw = dot(kv2[:, j * HD:(j + 1) * HD], qj, NT) * factor
        sown[j] = jnp.where(allow, raw, NEG_BIG)
        dpown[j] = dot(kv2[:, WIDTH + j * HD:WIDTH + (j + 1) * HD], gj, NT)

    ready(0)
    pl.semaphore_wait(barrier, n_grp - 1 + n_dp - 1)
    for j in range(KVH):
        exchange(*ag[j])
    for j in range(1, KVH):
        ready(j)

    for j in range(KVH):
        if j % STEP == 0:
            for k in range(j, j + STEP):
                arrived(*ag[k])
        kc = slice(j * HD, (j + 1) * HD)
        vc = slice(WIDTH + j * HD, WIDTH + (j + 1) * HD)
        both = pre_all[j].reshape(pre_rows, 2 * HD)
        pk = both[:, :HD]
        pv = both[:, HD:]
        qj = q2[j]
        gj = g2[j]
        s_p = dot(pk, qj, NT) * factor
        s_o = sown[j]
        dp_p = dot(pv, gj, NT)
        dp_o = dpown[j]
        top = jnp.maximum(jnp.max(s_p, 0, keepdims=True), jnp.max(s_o, 0, keepdims=True))
        e_p = jnp.exp(s_p - top)
        e_o = jnp.exp(s_o - top)
        inv = 1.0 / (jnp.sum(e_p, 0, keepdims=True) + jnp.sum(e_o, 0, keepdims=True))
        p_p = e_p * inv
        p_o = e_o * inv
        row = jnp.sum(p_p * dp_p, 0, keepdims=True) + jnp.sum(p_o * dp_o, 0, keepdims=True)
        ds = jnp.concatenate([(p_p * (dp_p - row)).astype(BF16), (p_o * (dp_o - row)).astype(BF16)], axis=0)
        pb = jnp.concatenate([p_p.astype(BF16), p_o.astype(BF16)], axis=0)
        pb_s[j] = pb
        keys = jnp.concatenate([pk, kv2[:, kc]], axis=0)
        dk = dot(ds, qj, NN) * factor
        dv = dot(pb, gj, NN)
        dq = dot(ds, keys, TN) * factor
        dkr = dk.astype(BF16)
        dvr = dv.astype(BF16)
        pg[j] = jnp.concatenate([dkr[:pre_rows], dvr[:pre_rows]], axis=1).reshape(n_grp, own_rows, 2 * HD)
        dkv_s[:, kc] = dkr[pre_rows:]
        dkv_s[:, vc] = dvr[pre_rows:]
        for at, grad in ((QH + j, dk), (QH + KVH + j, dv)):
            bs[at // rows_per, at % rows_per:at % rows_per + 1, :] = jnp.sum(grad, 0, keepdims=True)
        for h in range(GROUP):
            part = dq[h * slots:(h + 1) * slots]
            at = j * GROUP + h
            bs[at // rows_per, at % rows_per:at % rows_per + 1, :] = jnp.sum(part, 0, keepdims=True)
            dq_s[:, at * HD:(at + 1) * HD] = part.astype(BF16)
        if j == KVH - 1:
            exchange(*ba)
        if j % STEP == STEP - 1:
            for k in range(j + 1 - STEP, j + 1):
                exchange(*rs[k])

    def forward(j):
        pv = pre_all[j].reshape(pre_rows, 2 * HD)[:, HD:]
        vals = jnp.concatenate([pv, kv2[:, WIDTH + j * HD:WIDTH + (j + 1) * HD]], axis=0)
        out = dot(pb_s[j], vals, TN)
        for h in range(GROUP):
            at = j * GROUP + h
            att_s[:, at * HD:(at + 1) * HD] = jnp.where(live_out, out[h * slots:(h + 1) * slots], 0.0).astype(BF16)

    for j in range(KVH // 2):
        forward(j)

    arrived(*ba)
    br[me] = bs[me]
    total = br[0]
    for k in range(1, n_grp):
        total = total + br[k]
    b2[my] = total
    exchange(*bb)

    for j in range(KVH // 2, KVH):
        forward(j)

    for j in range(KVH):
        arrived(*rs[j])
        pr[j, me] = pg[j, me]
        acc = pr[j, 0].astype(F32)
        for k in range(1, n_grp):
            acc = acc + pr[j, k].astype(F32)
        acc = acc.astype(BF16)
        dpre_ref[:, j * HD:(j + 1) * HD] = acc[:, :HD]
        dpre_ref[:, WIDTH + j * HD:WIDTH + (j + 1) * HD] = acc[:, HD:]

    arrived(*bb)
    total = b2[0]
    for k in range(1, n_dp):
        total = total + b2[k]
    fin[me] = total
    exchange(*bc)
    for item in sent:
        item.wait_send()
    arrived(*bc)
    for r in range(QH):
        qsum_ref[pl.ds(r * HD, HD)] = fin[r // rows_per, r % rows_per]
    for r in range(2 * KVH):
        at = QH + r
        kvsum_ref[pl.ds(r * HD, HD)] = fin[at // rows_per, at % rows_per]


def write_out(*refs):
    count = (len(refs) - 1) // 2
    copies = [pltpu.make_async_copy(refs[k], refs[count + k], refs[-1].at[k]) for k in range(count)]
    for item in copies:
        item.start()
    for item in copies:
        item.wait()


def local(n_grp, n_dp, query, resp_kv, prefix_kv, query_bias, kv_bias, out_grad, lengths):
    slots = query.shape[1]
    own_rows = prefix_kv.shape[1]
    pre_rows = own_rows * n_grp
    rows_per = -(-(QH + 2 * KVH) // n_grp)
    if n_grp * 8 >= QH + 2 * KVH:
        rows_per = min(8, 1 << (rows_per - 1).bit_length())
    tile = -(-rows_per // 8) * 8
    qw = QH * HD
    kw = 2 * WIDTH
    hbm = pl.BlockSpec(memory_space=pltpu.HBM)
    vmem = pl.BlockSpec(memory_space=pltpu.VMEM)
    dma = lambda *n: pltpu.SemaphoreType.DMA(n)
    shapes = (
        jax.ShapeDtypeStruct((slots, qw), BF16),
        jax.ShapeDtypeStruct((slots, qw), BF16),
        jax.ShapeDtypeStruct((slots, kw), BF16),
        jax.ShapeDtypeStruct((own_rows, kw), BF16),
        jax.ShapeDtypeStruct((qw,), F32),
        jax.ShapeDtypeStruct((kw,), F32),
    )
    outs = pl.pallas_call(
        functools.partial(kernel, n_grp, n_dp, rows_per),
        name="replay",
        out_shape=shapes,
        in_specs=[pl.BlockSpec(memory_space=pltpu.SMEM)] + [hbm] * 6,
        out_specs=(vmem,) * 6,
        scratch_shapes=[
            pltpu.VMEM((own_rows, kw), BF16),
            pltpu.VMEM((qw,), F32),
            pltpu.VMEM((kw,), F32),
            pltpu.VMEM((slots, qw), BF16),
            pltpu.VMEM((slots, qw), BF16),
            pltpu.VMEM((slots, kw), BF16),
            pltpu.VMEM((KVH, GROUP * slots, HD), BF16),
            pltpu.VMEM((KVH, GROUP * slots, HD), BF16),
            pltpu.VMEM((slots, kw), BF16),
            pltpu.VMEM((KVH, slots, GROUP * slots), F32),
            pltpu.VMEM((KVH, slots, GROUP * slots), F32),
            pltpu.VMEM((KVH, pre_rows + slots, GROUP * slots), BF16),
            pltpu.VMEM((KVH, n_grp, own_rows, 2 * HD), BF16),
            pltpu.VMEM((KVH, n_grp, own_rows, 2 * HD), BF16),
            pltpu.VMEM((KVH, n_grp, own_rows, 2 * HD), BF16),
            pltpu.VMEM((n_grp, tile, HD), F32),
            pltpu.VMEM((n_grp, tile, HD), F32),
            pltpu.VMEM((n_dp, tile, HD), F32),
            pltpu.VMEM((n_grp, tile, HD), F32),
            dma(4 + 2 * KVH),
            dma(KVH, n_grp - 1), dma(KVH, n_grp), dma(KVH, n_grp - 1), dma(KVH, n_grp),
            dma(n_grp - 1), dma(n_grp), dma(n_dp - 1), dma(n_dp),
            dma(n_grp - 1), dma(n_grp),
        ],
        compiler_params=pltpu.CompilerParams(
            collective_id=0, has_side_effects=True, vmem_limit_bytes=24 * 1024 * 1024
        ),
    )(lengths, *(pltpu.with_memory_space_constraint(x, pltpu.HBM) for x in (query[0], resp_kv[0], prefix_kv[0], query_bias, kv_bias, out_grad[0])))
    att, dq, dkv, dpre, qsum, kvsum = pl.pallas_call(
        write_out,
        name="write_out",
        out_shape=shapes,
        in_specs=[vmem] * 6,
        out_specs=(hbm,) * 6,
        scratch_shapes=[dma(6)],
        compiler_params=pltpu.CompilerParams(vmem_limit_bytes=1024 * 1024),
    )(*outs)
    return att[None], dq[None], dkv[None], dpre[None], qsum, kvsum


def solution(mesh):
    return jax.shard_map(
        functools.partial(local, mesh.shape["grp"], mesh.shape["dp"]),
        mesh=mesh,
        in_specs=(
            P("dp", "grp", None),
            P("dp", "grp", None),
            P("dp", "grp", None),
            P(),
            P(),
            P("dp", "grp", None),
            P("dp", "grp"),
        ),
        out_specs=(
            P("dp", "grp", None),
            P("dp", "grp", None),
            P("dp", "grp", None),
            P("dp", "grp", None),
            P(),
            P(),
        ),
        check_vma=False,
    )
```

```python
import functools

import jax
import jax.numpy as jnp
from jax import lax
from jax.experimental import pallas as pl
from jax.experimental.pallas import tpu as pltpu
from jax.sharding import PartitionSpec as P

QH = 20
KVH = 4
STEP = 2
LOG2E = 1.4426950408889634
HD = 128
NEG_BIG = -1e30
GROUP = QH // KVH
WIDTH = KVH * HD
GCOLS = GROUP * HD
MESH = pl.DeviceIdType.MESH
F32 = jnp.float32
BF16 = jnp.bfloat16

NT = (((1,), (1,)), ((), ()))
NN = (((1,), (0,)), ((), ()))
TN = (((0,), (0,)), ((), ()))


def dot(a, b, dims):
    return lax.dot_general(a, b, dims, preferred_element_type=F32)


def heads_down(x):
    return jnp.concatenate([x[:, h * HD:(h + 1) * HD] for h in range(GROUP)], axis=0)


def prepare(
    n_grp,
    len_ref, q_hbm, kv_hbm, pre_hbm, qb_hbm, kvb_hbm, g_hbm,
    q2, g2, kv2, sown, dpown, pre_all,
    pre_ref, qb_ref, kvb_ref, q_s, g_s, kv_s, in_sem, ag_send, ag_recv,
):
    me = lax.axis_index("grp")
    factor = HD ** (-0.5)
    base2 = factor * LOG2E
    slots = q_s.shape[0]

    barrier = pltpu.get_barrier_semaphore()
    for off in range(1, n_grp):
        pl.semaphore_signal(barrier, inc=1, device_id={"grp": lax.rem(me + off, n_grp)}, device_id_type=MESH)
    base = 1 + 2 * KVH
    small = [
        pltpu.make_async_copy(src, dst, in_sem.at[base + k])
        for k, (src, dst) in enumerate(
            ((pre_hbm, pre_ref), (kvb_hbm, kvb_ref), (qb_hbm, qb_ref)))
    ]
    loads = [pltpu.make_async_copy(kv_hbm, kv_s, in_sem.at[0])]
    for j in range(KVH):
        cols = pl.ds(j * GCOLS, GCOLS)
        loads.append(pltpu.make_async_copy(q_hbm.at[:, cols], q_s.at[:, cols], in_sem.at[1 + 2 * j]))
        loads.append(pltpu.make_async_copy(g_hbm.at[:, cols], g_s.at[:, cols], in_sem.at[2 + 2 * j]))
    for item in small + loads:
        item.start()
    small[0].wait()
    small[1].wait()
    kvb = kvb_ref[...].reshape(1, 2 * WIDTH)
    mine = (pre_ref[...].astype(F32) + kvb).astype(BF16)
    for j in range(KVH):
        pre_all[j, me] = jnp.concatenate(
            [mine[:, j * HD:(j + 1) * HD], mine[:, WIDTH + j * HD:WIDTH + (j + 1) * HD]], axis=1)
    small[2].wait()

    sent = []

    def exchange(axis, here, count, src, dst, send, recv):
        for off in range(1, count):
            peer = lax.rem(here + off, count)
            sent.append(pltpu.make_async_remote_copy(
                src_ref=src(peer), dst_ref=dst.at[here],
                send_sem=send.at[off - 1], recv_sem=recv.at[here],
                device_id={axis: peer}, device_id_type=MESH))
            sent[-1].start()

    def arrived(axis, here, count, src, dst, send, recv):
        for off in range(1, count):
            peer = lax.rem(here + off, count)
            pltpu.make_async_remote_copy(
                src_ref=src(peer), dst_ref=dst.at[peer],
                send_sem=send.at[off - 1], recv_sem=recv.at[peer],
                device_id={axis: peer}, device_id_type=MESH).wait_recv()

    ag = [("grp", me, n_grp, lambda peer, j=j: pre_all.at[j, me], pre_all.at[j], ag_send.at[j], ag_recv.at[j])
          for j in range(KVH)]

    length = len_ref[0, 0]
    live_in = lax.broadcasted_iota(jnp.int32, (slots, GCOLS), 0) < length
    key_at = lax.broadcasted_iota(jnp.int32, (slots, slots), 0)
    row_at = lax.broadcasted_iota(jnp.int32, (slots, slots), 1)
    allow = jnp.concatenate([key_at <= row_at] * GROUP, axis=1)

    loads[0].wait()
    kv2[...] = (kv_s[...].astype(F32) + kvb).astype(BF16)
    qb = qb_ref[...].reshape(1, QH * HD)
    def ready(j):
        cols = slice(j * GCOLS, (j + 1) * GCOLS)
        loads[1 + 2 * j].wait()
        loads[2 + 2 * j].wait()
        qj = heads_down((q_s[:, cols].astype(F32) + qb[:, cols]).astype(BF16))
        gj = g_s[:, cols]
        gj = heads_down(jnp.where(live_in, gj, jnp.zeros_like(gj)))
        q2[j] = qj
        g2[j] = gj
        raw = dot(kv2[:, j * HD:(j + 1) * HD], qj, NT) * base2
        sown[j] = jnp.where(allow, raw, NEG_BIG)
        dpown[j] = dot(kv2[:, WIDTH + j * HD:WIDTH + (j + 1) * HD], gj, NT)

    ready(0)
    pl.semaphore_wait(barrier, n_grp - 1)
    for j in range(KVH):
        exchange(*ag[j])
    for j in range(1, KVH):
        ready(j)
    for j in range(KVH):
        arrived(*ag[j])
    for item in sent:
        item.wait_send()


def kernel(
    n_grp, n_dp, rows_per,
    len_ref, q2, g2, kv2, sown, dpown, pre_all,
    att_s, dq_s, dkv_s, dpre_ref, qsum_ref, kvsum_ref,
    pb_s, pg, pr, bs, br, b2, fin,
    pg_send, pg_recv, ba_send, ba_recv, bb_send, bb_recv, bc_send, bc_recv,
):
    me = lax.axis_index("grp")
    factor = HD ** (-0.5)
    base2 = factor * LOG2E
    my = lax.axis_index("dp")
    slots = kv2.shape[0]
    own_rows = dpre_ref.shape[0]
    pre_rows = n_grp * own_rows

    barrier = pltpu.get_barrier_semaphore()
    for off in range(1, n_grp):
        pl.semaphore_signal(barrier, inc=1, device_id={"grp": lax.rem(me + off, n_grp)}, device_id_type=MESH)
    for off in range(1, n_dp):
        pl.semaphore_signal(barrier, inc=1, device_id={"dp": lax.rem(my + off, n_dp)}, device_id_type=MESH)

    sent = []

    def exchange(axis, here, count, src, dst, send, recv):
        for off in range(1, count):
            peer = lax.rem(here + off, count)
            sent.append(pltpu.make_async_remote_copy(
                src_ref=src(peer), dst_ref=dst.at[here],
                send_sem=send.at[off - 1], recv_sem=recv.at[here],
                device_id={axis: peer}, device_id_type=MESH))
            sent[-1].start()

    def arrived(axis, here, count, src, dst, send, recv):
        for off in range(1, count):
            peer = lax.rem(here + off, count)
            pltpu.make_async_remote_copy(
                src_ref=src(peer), dst_ref=dst.at[peer],
                send_sem=send.at[off - 1], recv_sem=recv.at[peer],
                device_id={axis: peer}, device_id_type=MESH).wait_recv()

    rs = [("grp", me, n_grp, lambda peer, j=j: pg.at[j, peer], pr.at[j], pg_send.at[j], pg_recv.at[j])
          for j in range(KVH)]
    ba = ("grp", me, n_grp, lambda peer: bs.at[peer], br, ba_send, ba_recv)
    bb = ("dp", my, n_dp, lambda peer: b2.at[my], b2, bb_send, bb_recv)
    bc = ("grp", me, n_grp, lambda peer: fin.at[me], fin, bc_send, bc_recv)

    length = len_ref[0, 0]
    live_out = lax.broadcasted_iota(jnp.int32, (slots, HD), 0) < length

    for j in range(KVH):
        kc = slice(j * HD, (j + 1) * HD)
        vc = slice(WIDTH + j * HD, WIDTH + (j + 1) * HD)
        both = pre_all[j].reshape(pre_rows, 2 * HD)
        pk = both[:, :HD]
        pv = both[:, HD:]
        qj = q2[j]
        gj = g2[j]
        s_p = dot(pk, qj, NT) * base2
        s_o = sown[j]
        dp_p = dot(pv, gj, NT)
        dp_o = dpown[j]
        top = jnp.maximum(jnp.max(s_p, 0, keepdims=True), jnp.max(s_o, 0, keepdims=True))
        e_p = jnp.exp2(s_p - top)
        e_o = jnp.exp2(s_o - top)
        inv = 1.0 / (jnp.sum(e_p, 0, keepdims=True) + jnp.sum(e_o, 0, keepdims=True))
        p_p = e_p * inv
        p_o = e_o * inv
        row = jnp.sum(p_p * dp_p, 0, keepdims=True) + jnp.sum(p_o * dp_o, 0, keepdims=True)
        ds = jnp.concatenate([(p_p * (dp_p - row)).astype(BF16), (p_o * (dp_o - row)).astype(BF16)], axis=0)
        pb = jnp.concatenate([p_p.astype(BF16), p_o.astype(BF16)], axis=0)
        pb_s[j] = pb
        keys = jnp.concatenate([pk, kv2[:, kc]], axis=0)
        dk = dot(ds, qj, NN) * factor
        dv = dot(pb, gj, NN)
        dq = dot(ds, keys, TN) * factor
        dkr = dk.astype(BF16)
        dvr = dv.astype(BF16)
        pg[j] = jnp.concatenate([dkr[:pre_rows], dvr[:pre_rows]], axis=1).reshape(n_grp, own_rows, 2 * HD)
        dkv_s[:, kc] = dkr[pre_rows:]
        dkv_s[:, vc] = dvr[pre_rows:]
        for at, grad in ((QH + j, dk), (QH + KVH + j, dv)):
            bs[at // rows_per, at % rows_per:at % rows_per + 1, :] = jnp.sum(grad, 0, keepdims=True)
        for h in range(GROUP):
            part = dq[h * slots:(h + 1) * slots]
            at = j * GROUP + h
            bs[at // rows_per, at % rows_per:at % rows_per + 1, :] = jnp.sum(part, 0, keepdims=True)
            dq_s[:, at * HD:(at + 1) * HD] = part.astype(BF16)
        if j == STEP - 1:
            pl.semaphore_wait(barrier, n_grp - 1 + n_dp - 1)
        if j == KVH - 1:
            exchange(*ba)
        if j % STEP == STEP - 1:
            for k in range(j + 1 - STEP, j + 1):
                exchange(*rs[k])

    def forward(j):
        pv = pre_all[j].reshape(pre_rows, 2 * HD)[:, HD:]
        vals = jnp.concatenate([pv, kv2[:, WIDTH + j * HD:WIDTH + (j + 1) * HD]], axis=0)
        out = dot(pb_s[j], vals, TN)
        for h in range(GROUP):
            at = j * GROUP + h
            att_s[:, at * HD:(at + 1) * HD] = jnp.where(live_out, out[h * slots:(h + 1) * slots], 0.0).astype(BF16)

    for j in range(KVH // 2):
        forward(j)

    arrived(*ba)
    br[me] = bs[me]
    total = br[0]
    for k in range(1, n_grp):
        total = total + br[k]
    b2[my] = total
    exchange(*bb)

    for j in range(KVH // 2, KVH):
        forward(j)

    for j in range(KVH):
        arrived(*rs[j])
        pr[j, me] = pg[j, me]
        acc = pr[j, 0].astype(F32)
        for k in range(1, n_grp):
            acc = acc + pr[j, k].astype(F32)
        acc = acc.astype(BF16)
        dpre_ref[:, j * HD:(j + 1) * HD] = acc[:, :HD]
        dpre_ref[:, WIDTH + j * HD:WIDTH + (j + 1) * HD] = acc[:, HD:]

    arrived(*bb)
    total = b2[0]
    for k in range(1, n_dp):
        total = total + b2[k]
    fin[me] = total
    exchange(*bc)
    for item in sent:
        item.wait_send()
    arrived(*bc)
    for r in range(QH):
        qsum_ref[pl.ds(r * HD, HD)] = fin[r // rows_per, r % rows_per]
    for r in range(2 * KVH):
        at = QH + r
        kvsum_ref[pl.ds(r * HD, HD)] = fin[at // rows_per, at % rows_per]


def write_out(*refs):
    count = (len(refs) - 1) // 2
    copies = [pltpu.make_async_copy(refs[k], refs[count + k], refs[-1].at[k]) for k in range(count)]
    for item in copies:
        item.start()
    for item in copies:
        item.wait()


def local(n_grp, n_dp, query, resp_kv, prefix_kv, query_bias, kv_bias, out_grad, lengths):
    slots = query.shape[1]
    own_rows = prefix_kv.shape[1]
    pre_rows = own_rows * n_grp
    rows_per = -(-(QH + 2 * KVH) // n_grp)
    if n_grp * 8 >= QH + 2 * KVH:
        rows_per = min(8, 1 << (rows_per - 1).bit_length())
    tile = -(-rows_per // 8) * 8
    qw = QH * HD
    kw = 2 * WIDTH
    hbm = pl.BlockSpec(memory_space=pltpu.HBM)
    vmem = pl.BlockSpec(memory_space=pltpu.VMEM)
    dma = lambda *n: pltpu.SemaphoreType.DMA(n)
    shapes = (
        jax.ShapeDtypeStruct((slots, qw), BF16),
        jax.ShapeDtypeStruct((slots, qw), BF16),
        jax.ShapeDtypeStruct((slots, kw), BF16),
        jax.ShapeDtypeStruct((own_rows, kw), BF16),
        jax.ShapeDtypeStruct((qw,), F32),
        jax.ShapeDtypeStruct((kw,), F32),
    )
    v = jax.ShapeDtypeStruct
    side = GROUP * slots
    staged = (
        v((KVH, side, HD), BF16), v((KVH, side, HD), BF16), v((slots, kw), BF16),
        v((KVH, slots, side), F32), v((KVH, slots, side), F32), v((KVH, n_grp, own_rows, 2 * HD), BF16),
    )
    held = pl.pallas_call(
        functools.partial(prepare, n_grp),
        name="prepare",
        out_shape=staged,
        in_specs=[pl.BlockSpec(memory_space=pltpu.SMEM)] + [hbm] * 6,
        out_specs=(vmem,) * 6,
        scratch_shapes=[
            pltpu.VMEM((own_rows, kw), BF16),
            pltpu.VMEM((qw,), F32),
            pltpu.VMEM((kw,), F32),
            pltpu.VMEM((slots, qw), BF16),
            pltpu.VMEM((slots, qw), BF16),
            pltpu.VMEM((slots, kw), BF16),
            dma(4 + 2 * KVH), dma(KVH, n_grp - 1), dma(KVH, n_grp),
        ],
        compiler_params=pltpu.CompilerParams(
            collective_id=1, has_side_effects=True, vmem_limit_bytes=16 * 1024 * 1024
        ),
    )(lengths, *(pltpu.with_memory_space_constraint(x, pltpu.HBM) for x in (query[0], resp_kv[0], prefix_kv[0], query_bias, kv_bias, out_grad[0])))
    outs = pl.pallas_call(
        functools.partial(kernel, n_grp, n_dp, rows_per),
        name="replay",
        out_shape=shapes,
        in_specs=[pl.BlockSpec(memory_space=pltpu.SMEM)] + [vmem] * 6,
        out_specs=(vmem,) * 6,
        scratch_shapes=[
            pltpu.VMEM((KVH, pre_rows + slots, GROUP * slots), BF16),
            pltpu.VMEM((KVH, n_grp, own_rows, 2 * HD), BF16),
            pltpu.VMEM((KVH, n_grp, own_rows, 2 * HD), BF16),
            pltpu.VMEM((n_grp, tile, HD), F32),
            pltpu.VMEM((n_grp, tile, HD), F32),
            pltpu.VMEM((n_dp, tile, HD), F32),
            pltpu.VMEM((n_grp, tile, HD), F32),
            dma(KVH, n_grp - 1), dma(KVH, n_grp),
            dma(n_grp - 1), dma(n_grp), dma(n_dp - 1), dma(n_dp),
            dma(n_grp - 1), dma(n_grp),
        ],
        compiler_params=pltpu.CompilerParams(
            collective_id=0, has_side_effects=True, vmem_limit_bytes=24 * 1024 * 1024
        ),
    )(lengths, *held)
    att, dq, dkv, dpre, qsum, kvsum = pl.pallas_call(
        write_out,
        name="write_out",
        out_shape=shapes,
        in_specs=[vmem] * 6,
        out_specs=(hbm,) * 6,
        scratch_shapes=[dma(6)],
        compiler_params=pltpu.CompilerParams(vmem_limit_bytes=1024 * 1024),
    )(*outs)
    return att[None], dq[None], dkv[None], dpre[None], qsum, kvsum


def solution(mesh):
    return jax.shard_map(
        functools.partial(local, mesh.shape["grp"], mesh.shape["dp"]),
        mesh=mesh,
        in_specs=(
            P("dp", "grp", None),
            P("dp", "grp", None),
            P("dp", "grp", None),
            P(),
            P(),
            P("dp", "grp", None),
            P("dp", "grp"),
        ),
        out_specs=(
            P("dp", "grp", None),
            P("dp", "grp", None),
            P("dp", "grp", None),
            P("dp", "grp", None),
            P(),
            P(),
        ),
        check_vma=False,
    )
```
